32 devices in a mesh: dp: 8 (over y, x, core), tensor: 4 (over z).
Axes of the slice: x: 2, y: 2, z: 4, core: 2. Of those that a mesh axis runs over, the one named last changes fastest.
Arguments:
- tokens: bfloat16 [4096, 3072], P('dp', 'tensor'), may hold values from -6 to 6
- cotangent: bfloat16 [4096, 1024], P('dp'), may hold values from -8 to 8
- weight: bfloat16 [3072, 1024], P('tensor'), may hold values from -6 to 6
- momentum: bfloat16 [8, 3072, 1024], P('dp', 'tensor'), may hold values from -1.1953125 to 1.1953125
- threshold: int32 [1024], replicated, may hold values from 2 to 8
Outputs:
- key_values: bfloat16 [4096, 1024], P(('dp', 'tensor'))
- input_grad: bfloat16 [4096, 3072], P('dp', 'tensor')
- new_momentum: bfloat16 [8, 3072, 1024], P('dp', 'tensor')
- new_weight: bfloat16 [3072, 1024], P('tensor', 'dp')
The draws below stay inside these ranges and needn't reach their ends.
All inputs are finite; a program needn't handle non-finite values.
Results may differ from the reference program's by a relative error of at most 0.017.
Values may be sent and summed in bfloat16 or wider, within the bound.
No kernel may reach another device: no remote copies, remote signals or barrier semaphores. Data moves between devices by JAX's collectives and lax.ppermute only.
A program may use at most 64 MiB of HBM per device.

```python
import jax
import jax.numpy as jnp
from jax import lax

D = 3072
KVW = 1024
GROUP_ROWS = 512
TOKENS = 4096
N_DP = 8
N_TENSOR = 4


def place_ends(drawn, key, smallest, largest):
    spot = [jax.random.randint(jax.random.fold_in(key, axis), (), 0, length) for axis, length in enumerate(drawn.shape)]
    longest = drawn.shape.index(max(drawn.shape))
    neighbour = spot[:longest] + [(spot[longest] + 1) % drawn.shape[longest]] + spot[longest + 1:]
    return drawn.at[tuple(spot)].set(smallest).at[tuple(neighbour)].set(largest)


def strengthened(entries, key, source, target, blocks, factor):
    def block_of(dim):
        return (jnp.arange(entries.shape[dim]) // (entries.shape[dim] // blocks)).reshape((-1,) + (1,) * (entries.ndim - 1 - dim))

    near = jax.random.permutation(key, blocks)[block_of(target)]
    far = (block_of(target) + blocks // 2) % blocks
    return jnp.where((block_of(source) == near) | (block_of(source) == far), factor * entries, entries)


def shard_levels(key, shape, pieces, least, top_value):
    gain = 1.0
    for position, parts in pieces:
        heights = jax.random.uniform(jax.random.fold_in(jax.random.fold_in(key, 6), position), (parts,), jnp.float32, least / len(pieces), top_value / len(pieces))
        gain = gain * jnp.repeat(jnp.exp(heights), shape[position] // parts).reshape((-1,) + (1,) * (len(shape) - 1 - position))
    return gain


def bell_draw(rng, extent, scale, most, shards=(), dtype=jnp.bfloat16):
    result = jax.random.normal(rng, extent, jnp.float32) * scale
    if len(shards) > 0:
        result = shard_levels(rng, extent, shards, -0.22, 0.18) * result
    return jnp.clip(result, min=-most, max=most).astype(dtype)


def gaussian_with(key, dims, width, reach, shards, heavy, dtype=jnp.bfloat16):
    array = width * jax.random.normal(key, dims, jnp.float32)
    if shards:
        array = array * shard_levels(key, dims, shards, -0.22, 0.18)
    return jnp.clip(strengthened(array, jax.random.fold_in(key, 3), *heavy), -reach, reach).astype(dtype)


def setup_inputs(seed: int = 0) -> dict:
    key_list = jax.random.split(jax.random.key(seed), 6)
    tokens = bell_draw(key_list[0], (TOKENS, D), 1.0, 6.0, ((0, 8), (1, 4)))
    cotangent = bell_draw(key_list[1], (TOKENS, KVW), 1.0, 8.0, ((0, 8),))
    weight = bell_draw(key_list[2], (D, KVW), 1.0, 6.0, ((0, 4),))
    momentum = gaussian_with(key_list[3], (N_DP, D, KVW), 0.2, 1.1953125, ((0, 8), (1, 4)), (0, 2, 8, 2.0))
    threshold = place_ends(jax.random.randint(key_list[4], (KVW,), 2, 9), jax.random.fold_in(key_list[4], 1), 2, 8).astype(jnp.int32)
    return {"tokens": tokens, "cotangent": cotangent, "weight": weight, "momentum": momentum, "threshold": threshold}


def reference(tokens, cotangent, weight, momentum, threshold):
    inverse = D ** -0.5
    feature_share = D // N_TENSOR
    token_blocks = tokens.reshape(TOKENS, N_TENSOR, feature_share).transpose(1, 0, 2)
    weight_blocks = weight.reshape(N_TENSOR, feature_share, KVW)

    def add_partial(running, pair):
        token_block, weight_block = pair
        partial_value = jnp.dot(token_block, weight_block, preferred_element_type=jnp.float32) * inverse
        return running + partial_value.astype(jnp.bfloat16).astype(jnp.float32), None

    key_total, unused = lax.scan(add_partial, jnp.zeros((TOKENS, KVW), jnp.float32), (token_blocks, weight_blocks))
    key_values = key_total.astype(jnp.bfloat16)
    input_grad = (lax.dot_general(cotangent, weight, (((1,), (1,)), ((), ())), preferred_element_type=jnp.float32) * inverse).astype(jnp.bfloat16)
    token_groups = tokens.reshape(N_DP, GROUP_ROWS, D)
    cot_groups = cotangent.reshape(N_DP, GROUP_ROWS, KVW)

    def replica_step(votes, triple):
        group_tokens, group_cot, old_moment = triple
        gradient = lax.dot_general(group_tokens, group_cot, (((0,), (0,)), ((), ())), preferred_element_type=jnp.float32) * inverse
        fresh = (0.9 * old_moment.astype(jnp.float32) + 0.1 * gradient).astype(jnp.bfloat16)
        votes = votes + jnp.clip(fresh.astype(jnp.float32) / 0.125, -1.0, 1.0)
        return votes, fresh

    votes, new_momentum = lax.scan(replica_step, jnp.zeros((D, KVW), jnp.float32), (token_groups, cot_groups, momentum))
    update = jnp.clip(votes / threshold.astype(jnp.float32)[None, :], -1.0, 1.0)
    new_weight = (weight.astype(jnp.float32) - 0.5 * update).astype(jnp.bfloat16)
    return key_values, input_grad, new_momentum, new_weight
```

```python
import jax
import jax.numpy as jnp
from jax import lax
from jax.experimental import pallas as pl
from jax.experimental.pallas import tpu as pltpu
from jax.sharding import PartitionSpec as P

BF16 = jnp.bfloat16
F32 = jnp.float32
VMEM_LIMIT = 20 * 1024 * 1024
LANES = 128
WHOLE = pl.BlockSpec(memory_space=pltpu.VMEM)


def shaped(*dims):
    return jax.ShapeDtypeStruct(dims, BF16)


def params():
    return pltpu.CompilerParams(vmem_limit_bytes=VMEM_LIMIT)


def product_rows(tokens_ref, weight_ref, block, rows, inverse):
    picked = tokens_ref[pl.ds(pl.multiple_of(block * rows, rows), rows), :]
    total = jnp.dot(picked, weight_ref[...], preferred_element_type=F32)
    return (total * inverse).astype(BF16)


def is_outer(plane):
    return jnp.logical_or(plane == 0, plane == 3)


def far_block(plane):
    return jnp.where(plane % 2 == 0, 3, 0)


def near_block(plane):
    return jnp.where(plane % 2 == 0, 1, 2)


def third_block(plane):
    return jnp.where(plane == 0, 2, jnp.where(plane == 1, 3, jnp.where(plane == 2, 0, 1)))


def seed_kernel(inverse, rows, tokens_ref, weight_ref, out_ref):
    plane = lax.axis_index("tensor")
    out_ref[...] = product_rows(tokens_ref, weight_ref, far_block(plane), rows, inverse)


def rest_kernel(inverse, rows, tokens_ref, weight_ref, near_ref, third_ref, own_ref):
    plane = lax.axis_index("tensor")
    near_ref[...] = product_rows(tokens_ref, weight_ref, near_block(plane), rows, inverse)
    third_ref[...] = product_rows(tokens_ref, weight_ref, third_block(plane), rows, inverse)
    own_ref[...] = product_rows(tokens_ref, weight_ref, plane, rows, inverse)


def relay_kernel(third_ref, seed_ref, out_ref):
    outer = is_outer(lax.axis_index("tensor"))

    @pl.when(outer)
    def _():
        out_ref[...] = third_ref[...]

    @pl.when(jnp.logical_not(outer))
    def _():
        out_ref[...] = (third_ref[...].astype(F32) + seed_ref[...].astype(F32)).astype(BF16)


def keys_kernel(own_ref, seed_ref, across_ref, near_ref, third_ref, out_ref):
    outer = is_outer(lax.axis_index("tensor"))

    @pl.when(outer)
    def _():
        total = own_ref[...].astype(F32) + seed_ref[...].astype(F32)
        out_ref[...] = (total + third_ref[...].astype(F32)).astype(BF16)

    @pl.when(jnp.logical_not(outer))
    def _():
        total = own_ref[...].astype(F32) + across_ref[...].astype(F32)
        total = total + near_ref[...].astype(F32)
        out_ref[...] = (total + third_ref[...].astype(F32)).astype(BF16)


def momentum_kernel(inverse, share, tokens_ref, cot_ref, old_ref, new_ref, send_ref, keep_ref):
    odd = lax.axis_index("dp") % 2 == 1
    for pair in range(cot_ref.shape[1] // (2 * share)):
        span = slice(2 * pair * share, 2 * (pair + 1) * share)
        gradient = inverse * lax.dot_general(
            tokens_ref[...],
            cot_ref[:, span],
            (((0,), (0,)), ((), ())),
            preferred_element_type=F32,
        )
        fresh = (0.9 * old_ref[0, :, span].astype(F32) + 0.1 * gradient).astype(BF16)
        new_ref[0, :, span] = fresh
        votes = jnp.clip(fresh.astype(F32) * 8.0, -1.0, 1.0).astype(BF16)
        low, high = votes[:, :share], votes[:, share:]
        send_ref[pair] = jnp.where(odd, low, high)
        keep_ref[pair] = jnp.where(odd, high, low)


def pair_kernel(keep_ref, came_ref, *out_refs):
    chip = lax.axis_index("dp") // 2
    for offset, out_ref in enumerate(out_refs):
        there = jnp.bitwise_xor(chip, offset)
        total = keep_ref[there].astype(F32) + came_ref[there].astype(F32)
        out_ref[...] = total.astype(BF16)


def weight_kernel(share, weight_ref, threshold_ref, *refs):
    vote_refs, out_ref = refs[:-1], refs[-1]
    first = pl.multiple_of(lax.axis_index("dp") * share, share)
    votes = vote_refs[0][...].astype(F32)
    for ref in vote_refs[1:]:
        votes = votes + ref[...].astype(F32)
    limits = threshold_ref[:, pl.ds(first, share)].astype(F32)
    update = jnp.clip(votes / limits, -1.0, 1.0)
    old = weight_ref[:, pl.ds(first, share)].astype(F32)
    out_ref[...] = (old - 0.5 * update).astype(BF16)


def call(kernel, outs, *args, **more):
    more.setdefault("in_specs", [WHOLE] * len(args))
    more.setdefault("out_specs", [WHOLE] * len(outs))
    return pl.pallas_call(kernel, out_shape=outs, compiler_params=params(), **more)(*args)


def bind(function, *bound):
    def run(*refs):
        function(*bound, *refs)

    return run


def on_line_of_four(tokens, cotangent, weight, momentum, threshold):
    depth, width = weight.shape
    n_dp, n_tensor = lax.axis_size("dp"), lax.axis_size("tensor")
    rows = tokens.shape[0] // n_tensor
    share = width // n_dp
    inverse = (depth * n_tensor) ** (-0.5)

    def along(value, *pairs):
        return lax.ppermute(value, "tensor", pairs)

    def over(value, mask):
        return lax.ppermute(value, "dp", [(i, i ^ mask) for i in range(n_dp)])

    (seed,) = call(bind(seed_kernel, inverse, rows), [shaped(rows, width)], tokens, weight)
    seed_came = along(seed, (0, 1), (3, 2), (1, 0), (2, 3))

    tile = 256
    fresh, send, keep = call(
        bind(momentum_kernel, inverse, share),
        [
            shaped(1, depth, width),
            shaped(n_dp // 2, depth, share),
            shaped(n_dp // 2, depth, share),
        ],
        tokens,
        cotangent,
        momentum,
        grid=(depth // tile,),
        in_specs=[
            pl.BlockSpec((tokens.shape[0], tile), lambda i: (0, i)),
            pl.BlockSpec(cotangent.shape, lambda i: (0, 0)),
            pl.BlockSpec((1, tile, width), lambda i: (0, i, 0)),
        ],
        out_specs=[
            pl.BlockSpec((1, tile, width), lambda i: (0, i, 0)),
            pl.BlockSpec((n_dp // 2, tile, share), lambda i: (0, i, 0)),
            pl.BlockSpec((n_dp // 2, tile, share), lambda i: (0, i, 0)),
        ],
    )
    came = over(send, 1)

    near, third, own = call(
        bind(rest_kernel, inverse, rows), [shaped(rows, width)] * 3, tokens, weight
    )
    near_came = along(near, (0, 1), (3, 2), (1, 3), (2, 0))
    across_came = along(near, (1, 2), (2, 1), (0, 0), (3, 3))

    sums = call(bind(pair_kernel), [shaped(depth, share)] * (n_dp // 2), keep, came)
    votes = [sums[0]] + [over(sums[k], 2 * k) for k in range(1, n_dp // 2)]

    (relay,) = call(bind(relay_kernel), [shaped(rows, width)], third, seed_came)
    third_came = along(relay, (0, 2), (3, 1), (1, 3), (2, 0))

    input_grad = (
        lax.dot_general(cotangent, weight, (((1,), (1,)), ((), ())), preferred_element_type=F32)
        * inverse
    ).astype(BF16)

    (new_weight,) = call(
        bind(weight_kernel, share),
        [shaped(depth, share)],
        weight,
        threshold.reshape(1, width),
        *votes,
    )
    (key_values,) = call(
        bind(keys_kernel), [shaped(rows, width)], own, seed_came, across_came, near_came, third_came
    )
    return key_values, input_grad, fresh, new_weight


def in_general(tokens, cotangent, weight, momentum, threshold):
    inverse = (weight.shape[0] * lax.axis_size("tensor")) ** (-0.5)
    key_values = lax.psum_scatter(
        (jnp.dot(tokens, weight, preferred_element_type=F32) * inverse).astype(BF16),
        "tensor",
        scatter_dimension=0,
        tiled=True,
    )
    input_grad = (
        lax.dot_general(cotangent, weight, (((1,), (1,)), ((), ())), preferred_element_type=F32)
        * inverse
    ).astype(BF16)
    gradient = inverse * lax.dot_general(
        tokens, cotangent, (((0,), (0,)), ((), ())), preferred_element_type=F32
    )
    fresh = (0.9 * momentum[0].astype(F32) + 0.1 * gradient).astype(BF16)
    share = weight.shape[1] // lax.axis_size("dp")
    arrived = lax.all_to_all(fresh[None], "dp", split_axis=2, concat_axis=0, tiled=True)
    votes = jnp.sum(jnp.clip(arrived.astype(F32) / 0.125, -1.0, 1.0), axis=0)
    first = lax.axis_index("dp") * share
    own_columns = lax.dynamic_slice_in_dim(weight, first, share, 1)
    own_limits = lax.dynamic_slice_in_dim(threshold, first, share, 0)
    update = jnp.clip(votes / own_limits.astype(F32)[None, :], -1.0, 1.0)
    new_weight = (own_columns.astype(F32) - 0.5 * update).astype(BF16)
    return key_values, input_grad, fresh[None], new_weight


def per_device(tokens, cotangent, weight, momentum, threshold):
    depth, width = weight.shape
    n_dp, n_tensor = lax.axis_size("dp"), lax.axis_size("tensor")
    fits = n_tensor == 4 and n_dp in (4, 8) and width % (n_dp * LANES) == 0 and depth % 256 == 0
    chosen = on_line_of_four if fits else in_general
    return chosen(tokens, cotangent, weight, momentum, threshold)


def solution(mesh):
    in_specs = (P("dp", "tensor"), P("dp", None), P("tensor", None), P("dp", "tensor", None), P())
    out_specs = (
        P(("dp", "tensor"), None),
        P("dp", "tensor"),
        P("dp", "tensor", None),
        P("tensor", "dp"),
    )
    return jax.shard_map(
        per_device, mesh=mesh, in_specs=in_specs, out_specs=out_specs, check_vma=False
    )
```

```python
import jax
import jax.numpy as jnp
from jax import lax
from jax.experimental import pallas as pl
from jax.experimental.pallas import tpu as pltpu
from jax.sharding import PartitionSpec as P


BF16 = jnp.bfloat16
F32 = jnp.float32
VMEM_LIMIT = 20 * 1024 * 1024
LANES = 128
WHOLE = pl.BlockSpec(memory_space=pltpu.VMEM)


def shaped(*dims):
    return jax.ShapeDtypeStruct(dims, BF16)


def params():
    return pltpu.CompilerParams(vmem_limit_bytes=VMEM_LIMIT)


def product_rows(tokens_ref, weight_ref, block, rows, inverse):
    picked = tokens_ref[pl.ds(pl.multiple_of(block * rows, rows), rows), :]
    total = jnp.dot(picked, weight_ref[...], preferred_element_type=F32)
    return (total * inverse).astype(BF16)


def is_outer(plane):
    return jnp.logical_or(plane == 0, plane == 3)


def far_block(plane):
    return jnp.where(plane % 2 == 0, 3, 0)


def near_block(plane):
    return jnp.where(plane % 2 == 0, 1, 2)


def third_block(plane):
    return jnp.where(plane == 0, 2, jnp.where(plane == 1, 3, jnp.where(plane == 2, 0, 1)))


def seed_kernel(inverse, rows, tokens_ref, weight_ref, out_ref):
    plane = lax.axis_index("tensor")
    out_ref[...] = product_rows(tokens_ref, weight_ref, far_block(plane), rows, inverse)


def rest_kernel(inverse, rows, tokens_ref, weight_ref, near_ref, third_ref, own_ref):
    plane = lax.axis_index("tensor")
    near_ref[...] = product_rows(tokens_ref, weight_ref, near_block(plane), rows, inverse)
    third_ref[...] = product_rows(tokens_ref, weight_ref, third_block(plane), rows, inverse)
    own_ref[...] = product_rows(tokens_ref, weight_ref, plane, rows, inverse)


def relay_kernel(third_ref, seed_ref, out_ref):
    outer = is_outer(lax.axis_index("tensor"))

    @pl.when(outer)
    def _():
        out_ref[...] = third_ref[...]

    @pl.when(jnp.logical_not(outer))
    def _():
        out_ref[...] = (third_ref[...].astype(F32) + seed_ref[...].astype(F32)).astype(BF16)


def keys_kernel(own_ref, seed_ref, across_ref, near_ref, third_ref, out_ref):
    outer = is_outer(lax.axis_index("tensor"))

    @pl.when(outer)
    def _():
        total = own_ref[...].astype(F32) + seed_ref[...].astype(F32)
        out_ref[...] = (total + third_ref[...].astype(F32)).astype(BF16)

    @pl.when(jnp.logical_not(outer))
    def _():
        total = own_ref[...].astype(F32) + across_ref[...].astype(F32)
        total = total + near_ref[...].astype(F32)
        out_ref[...] = (total + third_ref[...].astype(F32)).astype(BF16)


def momentum_kernel(inverse, share, tokens_ref, cot_ref, old_ref, new_ref, send_ref, keep_ref):
    odd = lax.axis_index("dp") % 2 == 1
    for pair in range(cot_ref.shape[1] // (2 * share)):
        span = slice(2 * pair * share, 2 * (pair + 1) * share)
        gradient = inverse * lax.dot_general(
            tokens_ref[...],
            cot_ref[:, span],
            (((0,), (0,)), ((), ())),
            preferred_element_type=F32,
        )
        fresh = (0.9 * old_ref[0, :, span].astype(F32) + 0.1 * gradient).astype(BF16)
        new_ref[0, :, span] = fresh
        votes = jnp.clip(fresh.astype(F32) * 8.0, -1.0, 1.0).astype(BF16)
        low, high = votes[:, :share], votes[:, share:]
        send_ref[pair] = jnp.where(odd, low, high)
        keep_ref[pair] = jnp.where(odd, high, low)


def pair_kernel(keep_ref, came_ref, *out_refs):
    chip = lax.axis_index("dp") // 2
    for offset, out_ref in enumerate(out_refs):
        there = jnp.bitwise_xor(chip, offset)
        total = keep_ref[there].astype(F32) + came_ref[there].astype(F32)
        out_ref[...] = total.astype(BF16)


def weight_kernel(share, weight_ref, threshold_ref, *refs):
    vote_refs, out_ref = refs[:-1], refs[-1]
    first = pl.multiple_of(lax.axis_index("dp") * share, share)
    votes = vote_refs[0][...].astype(F32)
    for ref in vote_refs[1:]:
        votes = votes + ref[...].astype(F32)
    limits = threshold_ref[:, pl.ds(first, share)].astype(F32)
    update = jnp.clip(votes / limits, -1.0, 1.0)
    old = weight_ref[:, pl.ds(first, share)].astype(F32)
    out_ref[...] = (old - 0.5 * update).astype(BF16)


def call(kernel, outs, *args, **more):
    return run_kernel(kernel, outs, *args, **more)


def run_kernel(kernel, outs, *args, **more):
    more.setdefault("in_specs", [WHOLE] * len(args))
    more.setdefault("out_specs", [WHOLE] * len(outs))
    return pl.pallas_call(kernel, out_shape=outs, compiler_params=params(), **more)(*args)


def bind(function, *bound):
    def run(*refs):
        function(*bound, *refs)

    return run


def on_line_of_four(tokens, cotangent, weight, momentum, threshold):
    depth, width = weight.shape
    n_dp, n_tensor = lax.axis_size("dp"), lax.axis_size("tensor")
    rows = tokens.shape[0] // n_tensor
    share = width // n_dp
    inverse = (depth * n_tensor) ** (-0.5)

    def along(value, *pairs):
        return lax.ppermute(value, "tensor", pairs)

    def over(value, mask):
        return lax.ppermute(value, "dp", [(i, i ^ mask) for i in range(n_dp)])

    (seed,) = call(bind(seed_kernel, inverse, rows), [shaped(rows, width)], tokens, weight)
    seed_came = along(seed, (0, 1), (3, 2), (1, 0), (2, 3))

    tile = 256
    fresh, send, keep = call(bind(momentum_kernel, inverse, share),
        [
            shaped(1, depth, width),
            shaped(n_dp // 2, depth, share),
            shaped(n_dp // 2, depth, share),
        ],
        tokens,
        cotangent,
        momentum,
        grid=(depth // tile,),
        in_specs=[
            pl.BlockSpec((tokens.shape[0], tile), lambda i: (0, i)),
            pl.BlockSpec(cotangent.shape, lambda i: (0, 0)),
            pl.BlockSpec((1, tile, width), lambda i: (0, i, 0)),
        ],
        out_specs=[
            pl.BlockSpec((1, tile, width), lambda i: (0, i, 0)),
            pl.BlockSpec((n_dp // 2, tile, share), lambda i: (0, i, 0)),
            pl.BlockSpec((n_dp // 2, tile, share), lambda i: (0, i, 0)),
        ],
    )
    came = over(send, 1)

    near, third, own = call(bind(rest_kernel, inverse, rows), [shaped(rows, width)] * 3, tokens, weight
    )
    near_came = along(near, (0, 1), (3, 2))
    across_came = along(near, (1, 2), (2, 1), (0, 0), (3, 3))

    sums = call(bind(pair_kernel), [shaped(depth, share)] * (n_dp // 2), keep, came)
    farther = {k: over(sums[k], 2 * k) for k in reversed(range(1, n_dp // 2))}
    votes = [sums[0]] + [farther[k] for k in range(1, n_dp // 2)]

    (relay,) = call(bind(relay_kernel), [shaped(rows, width)], third, seed_came)
    third_came = along(relay, (0, 2), (3, 1), (1, 3), (2, 0))

    input_grad = lax.dot_general(
        cotangent, weight, (((1,), (1,)), ((), ())), preferred_element_type=F32
    )
    input_grad = (input_grad * inverse).astype(BF16)

    (new_weight,) = call(bind(weight_kernel, share),
        [shaped(depth, share)],
        weight,
        threshold.reshape(1, width),
        *votes,
    )
    (key_values,) = call(bind(keys_kernel), [shaped(rows, width)], own, seed_came, across_came, near_came, third_came
    )
    return key_values, input_grad, fresh, new_weight


def in_general(tokens, cotangent, weight, momentum, threshold):
    inverse = (weight.shape[0] * lax.axis_size("tensor")) ** (-0.5)
    key_values = lax.psum_scatter(
        (jnp.dot(tokens, weight, preferred_element_type=F32) * inverse).astype(BF16),
        "tensor",
        scatter_dimension=0,
        tiled=True,
    )
    input_grad = (
        lax.dot_general(cotangent, weight, (((1,), (1,)), ((), ())), preferred_element_type=F32)
        * inverse
    ).astype(BF16)
    gradient = inverse * lax.dot_general(
        tokens, cotangent, (((0,), (0,)), ((), ())), preferred_element_type=F32
    )
    fresh = (0.9 * momentum[0].astype(F32) + 0.1 * gradient).astype(BF16)
    share = weight.shape[1] // lax.axis_size("dp")
    arrived = lax.all_to_all(fresh[None], "dp", split_axis=2, concat_axis=0, tiled=True)
    votes = jnp.sum(jnp.clip(arrived.astype(F32) / 0.125, -1.0, 1.0), axis=0)
    first = lax.axis_index("dp") * share
    own_columns = lax.dynamic_slice_in_dim(weight, first, share, 1)
    own_limits = lax.dynamic_slice_in_dim(threshold, first, share, 0)
    update = jnp.clip(votes / own_limits.astype(F32)[None, :], -1.0, 1.0)
    new_weight = (own_columns.astype(F32) - 0.5 * update).astype(BF16)
    return key_values, input_grad, fresh[None], new_weight


def per_device(tokens, cotangent, weight, momentum, threshold):
    depth, width = weight.shape
    n_dp, n_tensor = lax.axis_size("dp"), lax.axis_size("tensor")
    fits = n_tensor == 4 and n_dp in (4, 8) and width % (n_dp * LANES) == 0 and depth % 256 == 0
    chosen = on_line_of_four if fits else in_general
    return chosen(tokens, cotangent, weight, momentum, threshold)


def solution(mesh):
    in_specs = (P("dp", "tensor"), P("dp", None), P("tensor", None), P("dp", "tensor", None), P())
    out_specs = (
        P(("dp", "tensor"), None),
        P("dp", "tensor"),
        P("dp", "tensor", None),
        P("tensor", "dp"),
    )
    return jax.shard_map(
        per_device, mesh=mesh, in_specs=in_specs, out_specs=out_specs, check_vma=False
    )
```

```python
import jax
import jax.numpy as jnp
from jax import lax
from jax.experimental import pallas as pl
from jax.experimental.pallas import tpu as pltpu
from jax.sharding import PartitionSpec as P


BF16 = jnp.bfloat16
F32 = jnp.float32
VMEM_LIMIT = 20 * 1024 * 1024
LANES = 128
TILE = 256
IN_VMEM = pl.BlockSpec(memory_space=pltpu.VMEM)
IN_HBM = pl.BlockSpec(memory_space=pltpu.HBM)


def shaped(*dims):
    return jax.ShapeDtypeStruct(dims, BF16)


def seed_block(plane):
    return jnp.where(plane % 2 == 0, 3, 0)


def near_block(plane):
    return jnp.where(plane % 2 == 0, 1, 2)


def third_block(plane):
    return jnp.where(plane == 0, 2, jnp.where(plane == 1, 3, jnp.where(plane == 2, 0, 1)))


def is_outer(plane):
    return jnp.logical_or(plane == 0, plane == 3)


def first_kernel(
    inverse,
    rows,
    tokens,
    weight,
    cotangent,
    seed_ref,
    near_ref,
    tokens_ref,
    weight_ref,
    cot_ref,
    sems,
):
    plane = lax.axis_index("tensor")
    blocks = (seed_block(plane), near_block(plane), third_block(plane), plane)
    spans = [pl.ds(pl.multiple_of(block * rows, rows), rows) for block in blocks]
    tiles = [pl.ds(k * TILE, TILE) for k in range(weight.shape[0] // TILE)]
    moves = [(tokens, tokens_ref, span) for span in spans[:2]]
    moves += [(weight, weight_ref, tile) for tile in tiles]
    moves += [(tokens, tokens_ref, span) for span in spans[2:]]
    moves += [(cotangent, cot_ref, pl.ds(0, cotangent.shape[0]))]
    copies = [
        pltpu.make_async_copy(source.at[span], goal.at[span], sems.at[k])
        for k, (source, goal, span) in enumerate(moves)
    ]
    for copy in copies:
        copy.start()
    copies[0].wait()
    copies[1].wait()
    held = jnp.concatenate([tokens_ref[spans[0], :], tokens_ref[spans[1], :]], axis=0)
    total = None
    for k in range(len(tiles)):
        copies[2 + k].wait()
        part = jnp.dot(
            held[:, k * TILE : (k + 1) * TILE],
            weight_ref[k * TILE : (k + 1) * TILE, :],
            preferred_element_type=F32,
        )
        total = part if total is None else total + part
    result = (total * inverse).astype(BF16)
    seed_ref[...] = result[:rows]
    near_ref[...] = result[rows:]
    for copy in copies[2 + len(tiles) :]:
        copy.wait()


def product_rows(tokens_ref, weight_ref, block, rows, inverse):
    picked = tokens_ref[pl.ds(pl.multiple_of(block * rows, rows), rows), :]
    total = jnp.dot(picked, weight_ref[...], preferred_element_type=F32)
    return (total * inverse).astype(BF16)


def rest_kernel(inverse, rows, tokens_ref, weight_ref, third_ref, own_ref):
    plane = lax.axis_index("tensor")
    third_ref[...] = product_rows(tokens_ref, weight_ref, third_block(plane), rows, inverse)
    own_ref[...] = product_rows(tokens_ref, weight_ref, plane, rows, inverse)


def relay_kernel(third_ref, near_ref, seed_ref, out_ref):
    outer = is_outer(lax.axis_index("tensor"))

    @pl.when(outer)
    def _():
        out_ref[...] = near_ref[...]

    @pl.when(jnp.logical_not(outer))
    def _():
        out_ref[...] = (third_ref[...].astype(F32) + seed_ref[...].astype(F32)).astype(BF16)


def momentum_kernel(step, share, tokens_ref, cot_ref, old_ref, fresh_ref, send_ref, keep_ref):
    odd = lax.axis_index("dp") % 2 == 1
    depth, width = fresh_ref.shape
    for k in range(depth // TILE):
        rows = slice(k * TILE, (k + 1) * TILE)
        turned = tokens_ref[:, rows].T
        for pair in range(width // (2 * share)):
            span = slice(2 * pair * share, 2 * (pair + 1) * share)
            gradient = jnp.dot(turned, cot_ref[:, span], preferred_element_type=F32)
            fresh = (0.9 * old_ref[0, rows, span].astype(F32) + step * gradient).astype(BF16)
            fresh_ref[rows, span] = fresh
            votes = jnp.clip(fresh * BF16(8), BF16(-1), BF16(1))
            low, high = votes[:, :share], votes[:, share:]
            send_ref[pair, rows] = jnp.where(odd, low, high)
            keep_ref[pair, rows] = jnp.where(odd, high, low)


def back_kernel(inverse, cot_ref, weight_ref, fresh_ref, back, new, back_ref, sems):
    store = pltpu.make_async_copy(fresh_ref, new.at[0], sems.at[0])
    store.start()
    rows = cot_ref.shape[0] // 2
    stores = [store]
    for k in range(2):
        span = pl.ds(k * rows, rows)
        total = lax.dot_general(
            cot_ref[k * rows : (k + 1) * rows, :],
            weight_ref[...],
            (((1,), (1,)), ((), ())),
            preferred_element_type=F32,
        )
        back_ref[k * rows : (k + 1) * rows, :] = (total * inverse).astype(BF16)
        stores.append(pltpu.make_async_copy(back_ref.at[span], back.at[span], sems.at[1 + k]))
        stores[-1].start()
    for store in stores:
        store.wait()


def pair_kernel(keep_ref, came_ref, *out_refs):
    chip = lax.axis_index("dp") // 2
    for offset, out_ref in enumerate(out_refs):
        there = jnp.bitwise_xor(chip, offset)
        total = keep_ref[there].astype(F32) + came_ref[there].astype(F32)
        out_ref[...] = total.astype(BF16)


def finish_kernel(
    share,
    own_ref,
    seed_ref,
    cross_ref,
    cycle_ref,
    last_ref,
    weight_ref,
    threshold_ref,
    *refs,
):
    vote_refs, (new_weight, keys, weight_out, keys_out, sems) = refs[:-5], refs[-5:]
    first = pl.multiple_of(lax.axis_index("dp") * share, share)
    votes = vote_refs[0][...].astype(F32)
    for ref in vote_refs[1:]:
        votes = votes + ref[...].astype(F32)
    limits = threshold_ref[:, pl.ds(first, share)].astype(F32)
    update = jnp.clip(votes / limits, -1.0, 1.0)
    old = weight_ref[:, pl.ds(first, share)].astype(F32)
    weight_out[...] = (old - 0.5 * update).astype(BF16)
    weight_copy = pltpu.make_async_copy(weight_out, new_weight, sems.at[0])
    weight_copy.start()

    outer = is_outer(lax.axis_index("tensor"))
    total = own_ref[...].astype(F32) + last_ref[...].astype(F32)

    @pl.when(outer)
    def _():
        keys_out[...] = (total + seed_ref[...].astype(F32)).astype(BF16)

    @pl.when(jnp.logical_not(outer))
    def _():
        more = cross_ref[...].astype(F32) + cycle_ref[...].astype(F32)
        keys_out[...] = (total + more).astype(BF16)

    keys_copy = pltpu.make_async_copy(keys_out, keys, sems.at[1])
    keys_copy.start()
    weight_copy.wait()
    keys_copy.wait()


def in_hbm(array):
    return pltpu.with_memory_space_constraint(array, pltpu.HBM)


def call(kernel, bound, outs, args, in_specs=None, out_specs=None, scratch=(), limit=VMEM_LIMIT):
    def body(*refs):
        kernel(*bound, *refs)

    return pl.pallas_call(
        body,
        out_shape=outs,
        in_specs=in_specs or [IN_VMEM] * len(args),
        out_specs=out_specs or [IN_VMEM] * len(outs),
        scratch_shapes=scratch,
        compiler_params=pltpu.CompilerParams(vmem_limit_bytes=limit),
    )(*args)


def on_line_of_four(tokens, cotangent, weight, momentum, threshold):
    depth, width = weight.shape
    n_dp, n_tensor = lax.axis_size("dp"), lax.axis_size("tensor")
    n_chips = n_dp // 2
    rows = tokens.shape[0] // n_tensor
    share = width // n_dp
    inverse = (depth * n_tensor) ** (-0.5)
    dma = pltpu.SemaphoreType.DMA

    def along(value, goal):
        pairs = []
        for d in range(n_dp):
            for plane in range(n_tensor):
                to = goal[plane]
                there = d * n_tensor + to if to is not None else (d ^ 1) * n_tensor + plane
                pairs.append((d * n_tensor + plane, there))
        return lax.ppermute(value, ("dp", "tensor"), pairs)

    def over(value, mask):
        return lax.ppermute(value, "dp", [(i, i ^ mask) for i in range(n_dp)])

    block = shaped(rows, width)
    seed, near, tokens, weight, cotangent = call(
        first_kernel,
        (inverse, rows),
        [block, block, shaped(*tokens.shape), shaped(*weight.shape), shaped(*cotangent.shape)],
        (in_hbm(tokens), in_hbm(weight), in_hbm(cotangent)),
        in_specs=[IN_HBM] * 3,
        scratch=[dma((5 + depth // TILE,))],
    )
    seed_came = along(seed, (1, 0, 3, 2))
    cross_came = along(near, (None, 2, 1, None))

    votes_shape = shaped(n_chips, depth, share)
    fresh, send, keep = call(
        momentum_kernel,
        (0.1 * inverse, share),
        [shaped(depth, width), votes_shape, votes_shape],
        (tokens, cotangent, momentum),
    )
    came = over(send, 1)

    third, own = call(rest_kernel, (inverse, rows), [block] * 2, (tokens, weight))
    cycle_came = along(third, (2, 0, 3, 1))

    sums = call(pair_kernel, (), [shaped(depth, share)] * n_chips, (keep, came))
    votes = [sums[0]] + [over(sums[k], 2 * k) for k in range(1, n_chips)]

    (relay,) = call(relay_kernel, (), [block], (third, near, seed_came))
    last_came = along(relay, (1, 3, 0, 2))

    input_grad, new_momentum = call(
        back_kernel,
        (inverse,),
        [shaped(*tokens.shape), shaped(1, depth, width)],
        (cotangent, weight, fresh),
        out_specs=[IN_HBM] * 2,
        scratch=[pltpu.VMEM(tokens.shape, BF16), dma((3,))],
    )
    new_weight, key_values = call(
        finish_kernel,
        (share,),
        [shaped(depth, share), block],
        (own, seed_came, cross_came, cycle_came, last_came, weight, threshold.reshape(1, width))
        + tuple(votes),
        out_specs=[IN_HBM] * 2,
        scratch=[pltpu.VMEM((depth, share), BF16), pltpu.VMEM((rows, width), BF16), dma((2,))],
    )
    return key_values, input_grad, new_momentum, new_weight


def in_general(tokens, cotangent, weight, momentum, threshold):
    inverse = (weight.shape[0] * lax.axis_size("tensor")) ** (-0.5)
    key_values = lax.psum_scatter(
        (jnp.dot(tokens, weight, preferred_element_type=F32) * inverse).astype(BF16),
        "tensor",
        scatter_dimension=0,
        tiled=True,
    )
    input_grad = (
        lax.dot_general(cotangent, weight, (((1,), (1,)), ((), ())), preferred_element_type=F32)
        * inverse
    ).astype(BF16)
    gradient = inverse * lax.dot_general(
        tokens, cotangent, (((0,), (0,)), ((), ())), preferred_element_type=F32
    )
    fresh = (0.9 * momentum[0].astype(F32) + 0.1 * gradient).astype(BF16)
    share = weight.shape[1] // lax.axis_size("dp")
    arrived = lax.all_to_all(fresh[None], "dp", split_axis=2, concat_axis=0, tiled=True)
    votes = jnp.sum(jnp.clip(arrived.astype(F32) / 0.125, -1.0, 1.0), axis=0)
    first = lax.axis_index("dp") * share
    own_columns = lax.dynamic_slice_in_dim(weight, first, share, 1)
    own_limits = lax.dynamic_slice_in_dim(threshold, first, share, 0)
    update = jnp.clip(votes / own_limits.astype(F32)[None, :], -1.0, 1.0)
    new_weight = (own_columns.astype(F32) - 0.5 * update).astype(BF16)
    return key_values, input_grad, fresh[None], new_weight


def solution(mesh):
    n_dp, n_tensor = mesh.shape["dp"], mesh.shape["tensor"]

    def per_device(tokens, cotangent, weight, momentum, threshold):
        depth, width = weight.shape
        fits = n_tensor == 4 and n_dp == 8 and width % (n_dp * LANES) == 0 and depth % TILE == 0
        chosen = on_line_of_four if fits else in_general
        return chosen(tokens, cotangent, weight, momentum, threshold)

    in_specs = (P("dp", "tensor"), P("dp", None), P("tensor", None), P("dp", "tensor", None), P())
    out_specs = (
        P(("dp", "tensor"), None),
        P("dp", "tensor"),
        P("dp", "tensor", None),
        P("tensor", "dp"),
    )
    return jax.shard_map(
        per_device, mesh=mesh, in_specs=in_specs, out_specs=out_specs, check_vma=False
    )
```

```python
import jax
import jax.numpy as jnp
from jax import lax
from jax.experimental import pallas as pl
from jax.experimental.pallas import tpu as pltpu
from jax.sharding import PartitionSpec as P


BF16 = jnp.bfloat16
F32 = jnp.float32
VMEM_LIMIT = 20 * 1024 * 1024
LANES = 128
TILE = 256
IN_VMEM = pl.BlockSpec(memory_space=pltpu.VMEM)
IN_HBM = pl.BlockSpec(memory_space=pltpu.HBM)


def shaped(*dims):
    return jax.ShapeDtypeStruct(dims, BF16)


def seed_block(plane):
    return jnp.where(plane % 2 == 0, 3, 0)


def near_block(plane):
    return jnp.where(plane % 2 == 0, 1, 2)


def third_block(plane):
    return jnp.where(plane == 0, 2, jnp.where(plane == 1, 3, jnp.where(plane == 2, 0, 1)))


def is_outer(plane):
    return jnp.logical_or(plane == 0, plane == 3)


def first_kernel(
    inverse,
    rows,
    tokens,
    weight,
    cotangent,
    seed_ref,
    near_ref,
    tokens_ref,
    weight_ref,
    cot_ref,
    sems,
):
    plane = lax.axis_index("tensor")
    blocks = (seed_block(plane), near_block(plane), third_block(plane), plane)
    spans = [pl.ds(pl.multiple_of(block * rows, rows), rows) for block in blocks]
    tiles = [pl.ds(k * TILE, TILE) for k in range(weight.shape[0] // TILE)]
    moves = [(tokens, tokens_ref, span) for span in spans[:2]]
    moves += [(weight, weight_ref, tile) for tile in tiles]
    moves += [(tokens, tokens_ref, span) for span in spans[2:]]
    moves += [(cotangent, cot_ref, pl.ds(0, cotangent.shape[0]))]
    copies = [
        pltpu.make_async_copy(source.at[span], goal.at[span], sems.at[k])
        for k, (source, goal, span) in enumerate(moves)
    ]
    for copy in copies:
        copy.start()
    copies[0].wait()
    copies[1].wait()
    held = jnp.concatenate([tokens_ref[spans[0], :], tokens_ref[spans[1], :]], axis=0)
    total = None
    for k in range(len(tiles)):
        copies[2 + k].wait()
        part = jnp.dot(
            held[:, k * TILE : (k + 1) * TILE],
            weight_ref[k * TILE : (k + 1) * TILE, :],
            preferred_element_type=F32,
        )
        total = part if total is None else total + part
    result = (total * inverse).astype(BF16)
    seed_ref[...] = result[:rows]
    near_ref[...] = result[rows:]
    for copy in copies[2 + len(tiles) :]:
        copy.wait()


def product_rows(tokens_ref, weight_ref, block, rows, inverse):
    picked = tokens_ref[pl.ds(pl.multiple_of(block * rows, rows), rows), :]
    total = jnp.dot(picked, weight_ref[...], preferred_element_type=F32)
    return (total * inverse).astype(BF16)


def rest_kernel(inverse, rows, tokens_ref, weight_ref, third_ref, own_ref):
    plane = lax.axis_index("tensor")
    third_ref[...] = product_rows(tokens_ref, weight_ref, third_block(plane), rows, inverse)
    own_ref[...] = product_rows(tokens_ref, weight_ref, plane, rows, inverse)


def relay_kernel(third_ref, near_ref, seed_ref, out_ref):
    outer = is_outer(lax.axis_index("tensor"))

    @pl.when(outer)
    def _():
        out_ref[...] = near_ref[...]

    @pl.when(jnp.logical_not(outer))
    def _():
        out_ref[...] = (third_ref[...].astype(F32) + seed_ref[...].astype(F32)).astype(BF16)


def momentum_kernel(step, share, tokens_ref, cot_ref, old_ref, fresh_ref, send_ref, keep_ref):
    odd = lax.axis_index("dp") % 2 == 1
    depth, width = fresh_ref.shape
    for k in range(depth // TILE):
        rows = slice(k * TILE, (k + 1) * TILE)
        turned = tokens_ref[:, rows].T
        for pair in range(width // (2 * share)):
            span = slice(2 * pair * share, 2 * (pair + 1) * share)
            gradient = jnp.dot(turned, cot_ref[:, span], preferred_element_type=F32)
            fresh = (0.9 * old_ref[0, rows, span].astype(F32) + step * gradient).astype(BF16)
            fresh_ref[rows, span] = fresh
            votes = jnp.clip(fresh * BF16(8), BF16(-1), BF16(1))
            low, high = votes[:, :share], votes[:, share:]
            send_ref[pair, rows] = jnp.where(odd, low, high)
            keep_ref[pair, rows] = jnp.where(odd, high, low)


def back_kernel(inverse, cot_ref, weight_ref, fresh_ref, back, new, back_ref, sems):
    store = pltpu.make_async_copy(fresh_ref, new.at[0], sems.at[0])
    store.start()
    rows = cot_ref.shape[0] // 2
    stores = [store]
    for k in range(2):
        span = pl.ds(k * rows, rows)
        total = lax.dot_general(
            cot_ref[k * rows : (k + 1) * rows, :],
            weight_ref[...],
            (((1,), (1,)), ((), ())),
            preferred_element_type=F32,
        )
        back_ref[k * rows : (k + 1) * rows, :] = (total * inverse).astype(BF16)
        stores.append(pltpu.make_async_copy(back_ref.at[span], back.at[span], sems.at[1 + k]))
        stores[-1].start()
    for store in stores:
        store.wait()


def pair_kernel(keep_ref, came_ref, *out_refs):
    place = lax.axis_index("dp")
    for step, out_ref in enumerate(out_refs):
        there = jnp.bitwise_xor(place // 2, chip_offset(place, step))
        total = keep_ref[there].astype(F32) + came_ref[there].astype(F32)
        out_ref[...] = total.astype(BF16)


def chip_offset(place, step):
    return step if step in (0, 3) else 1 + (step - 1 + place) % 2


def update_kernel(share, weight_ref, threshold_ref, *refs):
    vote_refs, out_ref = refs[:-1], refs[-1]
    first = pl.multiple_of(lax.axis_index("dp") * share, share)
    votes = vote_refs[0][...].astype(F32)
    for ref in vote_refs[1:]:
        votes = votes + ref[...].astype(F32)
    limits = threshold_ref[:, pl.ds(first, share)].astype(F32)
    update = jnp.clip(votes / limits, -1.0, 1.0)
    old = weight_ref[:, pl.ds(first, share)].astype(F32)
    out_ref[...] = (old - 0.5 * update).astype(BF16)


def keys_kernel(
    own_ref,
    seed_ref,
    cross_ref,
    cycle_ref,
    last_ref,
    updated_ref,
    keys,
    new_weight,
    keys_ref,
    sems,
):
    weight_copy = pltpu.make_async_copy(updated_ref, new_weight, sems.at[0])
    weight_copy.start()
    outer = is_outer(lax.axis_index("tensor"))
    total = own_ref[...].astype(F32) + last_ref[...].astype(F32)

    @pl.when(outer)
    def _():
        keys_ref[...] = (total + seed_ref[...].astype(F32)).astype(BF16)

    @pl.when(jnp.logical_not(outer))
    def _():
        more = cross_ref[...].astype(F32) + cycle_ref[...].astype(F32)
        keys_ref[...] = (total + more).astype(BF16)

    keys_copy = pltpu.make_async_copy(keys_ref, keys, sems.at[1])
    keys_copy.start()
    weight_copy.wait()
    keys_copy.wait()


def in_hbm(array):
    return pltpu.with_memory_space_constraint(array, pltpu.HBM)


def call(kernel, bound, outs, args, in_specs=None, out_specs=None, scratch=(), limit=VMEM_LIMIT):
    def body(*refs):
        kernel(*bound, *refs)

    return pl.pallas_call(
        body,
        out_shape=outs,
        in_specs=in_specs or [IN_VMEM] * len(args),
        out_specs=out_specs or [IN_VMEM] * len(outs),
        scratch_shapes=scratch,
        compiler_params=pltpu.CompilerParams(vmem_limit_bytes=limit),
    )(*args)


def on_line_of_four(tokens, cotangent, weight, momentum, threshold):
    depth, width = weight.shape
    n_dp, n_tensor = lax.axis_size("dp"), lax.axis_size("tensor")
    n_chips = n_dp // 2
    rows = tokens.shape[0] // n_tensor
    share = width // n_dp
    inverse = (depth * n_tensor) ** (-0.5)
    dma = pltpu.SemaphoreType.DMA

    def along(value, goal):
        pairs = []
        for d in range(n_dp):
            for plane in range(n_tensor):
                to = goal[plane]
                there = d * n_tensor + to if to is not None else (d ^ 1) * n_tensor + plane
                pairs.append((d * n_tensor + plane, there))
        return lax.ppermute(value, ("dp", "tensor"), pairs)

    def over(value, goal):
        return lax.ppermute(value, "dp", [(i, goal(i)) for i in range(n_dp)])

    block = shaped(rows, width)
    seed, near, tokens, weight, cotangent = call(
        first_kernel,
        (inverse, rows),
        [block, block, shaped(*tokens.shape), shaped(*weight.shape), shaped(*cotangent.shape)],
        (in_hbm(tokens), in_hbm(weight), in_hbm(cotangent)),
        in_specs=[IN_HBM] * 3,
        scratch=[dma((5 + depth // TILE,))],
    )
    seed_came = along(seed, (1, 0, 3, 2))
    cross_came = along(near, (None, 2, 1, None))

    votes_shape = shaped(n_chips, depth, share)
    fresh, send, keep = call(
        momentum_kernel,
        (0.1 * inverse, share),
        [shaped(depth, width), votes_shape, votes_shape],
        (tokens, cotangent, momentum),
    )
    came = over(send, lambda i: i ^ 1)

    third, own = call(rest_kernel, (inverse, rows), [block] * 2, (tokens, weight))
    cycle_came = along(third, (2, 0, 3, 1))

    sums = call(pair_kernel, (), [shaped(depth, share)] * n_chips, (keep, came))
    votes = [sums[0]] + [
        over(sums[k], lambda i, k=k: i ^ (2 * chip_offset(i, k)))
        for k in range(1, n_chips)
    ]

    (relay,) = call(relay_kernel, (), [block], (third, near, seed_came))
    last_came = along(relay, (1, 3, 0, 2))

    input_grad, new_momentum = call(
        back_kernel,
        (inverse,),
        [shaped(*tokens.shape), shaped(1, depth, width)],
        (cotangent, weight, fresh),
        out_specs=[IN_HBM] * 2,
        scratch=[pltpu.VMEM(tokens.shape, BF16), dma((3,))],
    )
    (updated,) = call(
        update_kernel,
        (share,),
        [shaped(depth, share)],
        (weight, threshold.reshape(1, width)) + tuple(votes),
    )
    key_values, new_weight = call(
        keys_kernel,
        (),
        [block, shaped(depth, share)],
        (own, seed_came, cross_came, cycle_came, last_came, updated),
        out_specs=[IN_HBM] * 2,
        scratch=[pltpu.VMEM((rows, width), BF16), dma((2,))],
    )
    return key_values, input_grad, new_momentum, new_weight


def in_general(tokens, cotangent, weight, momentum, threshold):
    inverse = (weight.shape[0] * lax.axis_size("tensor")) ** (-0.5)
    key_values = lax.psum_scatter(
        (jnp.dot(tokens, weight, preferred_element_type=F32) * inverse).astype(BF16),
        "tensor",
        scatter_dimension=0,
        tiled=True,
    )
    input_grad = (
        lax.dot_general(cotangent, weight, (((1,), (1,)), ((), ())), preferred_element_type=F32)
        * inverse
    ).astype(BF16)
    gradient = inverse * lax.dot_general(
        tokens, cotangent, (((0,), (0,)), ((), ())), preferred_element_type=F32
    )
    fresh = (0.9 * momentum[0].astype(F32) + 0.1 * gradient).astype(BF16)
    share = weight.shape[1] // lax.axis_size("dp")
    arrived = lax.all_to_all(fresh[None], "dp", split_axis=2, concat_axis=0, tiled=True)
    votes = jnp.sum(jnp.clip(arrived.astype(F32) / 0.125, -1.0, 1.0), axis=0)
    first = lax.axis_index("dp") * share
    own_columns = lax.dynamic_slice_in_dim(weight, first, share, 1)
    own_limits = lax.dynamic_slice_in_dim(threshold, first, share, 0)
    update = jnp.clip(votes / own_limits.astype(F32)[None, :], -1.0, 1.0)
    new_weight = (own_columns.astype(F32) - 0.5 * update).astype(BF16)
    return key_values, input_grad, fresh[None], new_weight


def solution(mesh):
    n_dp, n_tensor = mesh.shape["dp"], mesh.shape["tensor"]

    def per_device(tokens, cotangent, weight, momentum, threshold):
        depth, width = weight.shape
        fits = n_tensor == 4 and n_dp == 8 and width % (n_dp * LANES) == 0 and depth % TILE == 0
        chosen = on_line_of_four if fits else in_general
        return chosen(tokens, cotangent, weight, momentum, threshold)

    in_specs = (P("dp", "tensor"), P("dp", None), P("tensor", None), P("dp", "tensor", None), P())
    out_specs = (
        P(("dp", "tensor"), None),
        P("dp", "tensor"),
        P("dp", "tensor", None),
        P("tensor", "dp"),
    )
    return jax.shard_map(
        per_device, mesh=mesh, in_specs=in_specs, out_specs=out_specs, check_vma=False
    )
```

```python
import jax
import jax.numpy as jnp
from jax import lax
from jax.experimental import pallas as pl
from jax.experimental.pallas import tpu as pltpu
from jax.sharding import PartitionSpec as P


BF16 = jnp.bfloat16
F32 = jnp.float32
VMEM_LIMIT = 20 * 1024 * 1024
LANES = 128
TILE = 256
IN_VMEM = pl.BlockSpec(memory_space=pltpu.VMEM)
IN_HBM = pl.BlockSpec(memory_space=pltpu.HBM)


def shaped(*dims):
    return jax.ShapeDtypeStruct(dims, BF16)


def seed_block(plane):
    return jnp.where(plane % 2 == 0, 3, 0)


def near_block(plane):
    return jnp.where(plane % 2 == 0, 1, 2)


def third_block(plane):
    return jnp.where(plane == 0, 2, jnp.where(plane == 1, 3, jnp.where(plane == 2, 0, 1)))


def is_outer(plane):
    return jnp.logical_or(plane == 0, plane == 3)


def first_kernel(
    inverse,
    rows,
    tokens,
    weight,
    cotangent,
    seed_ref,
    near_ref,
    tokens_ref,
    weight_ref,
    cot_ref,
    sems,
):
    plane = lax.axis_index("tensor")
    blocks = (seed_block(plane), near_block(plane), third_block(plane), plane)
    spans = [pl.ds(pl.multiple_of(block * rows, rows), rows) for block in blocks]
    tiles = [pl.ds(k * TILE, TILE) for k in range(weight.shape[0] // TILE)]
    moves = [(tokens, tokens_ref, span) for span in spans[:2]]
    moves += [(weight, weight_ref, tile) for tile in tiles]
    moves += [(tokens, tokens_ref, span) for span in spans[2:]]
    moves += [(cotangent, cot_ref, pl.ds(0, cotangent.shape[0]))]
    copies = [
        pltpu.make_async_copy(source.at[span], goal.at[span], sems.at[k])
        for k, (source, goal, span) in enumerate(moves)
    ]
    for copy in copies:
        copy.start()
    copies[0].wait()
    copies[1].wait()
    held = jnp.concatenate([tokens_ref[spans[0], :], tokens_ref[spans[1], :]], axis=0)
    total = None
    for k in range(len(tiles)):
        copies[2 + k].wait()
        part = jnp.dot(
            held[:, k * TILE : (k + 1) * TILE],
            weight_ref[k * TILE : (k + 1) * TILE, :],
            preferred_element_type=F32,
        )
        total = part if total is None else total + part
    result = (total * inverse).astype(BF16)
    seed_ref[...] = result[:rows]
    near_ref[...] = result[rows:]
    for copy in copies[2 + len(tiles) :]:
        copy.wait()


def product_rows(tokens_ref, weight_ref, block, rows, inverse):
    picked = tokens_ref[pl.ds(pl.multiple_of(block * rows, rows), rows), :]
    total = jnp.dot(picked, weight_ref[...], preferred_element_type=F32)
    return (total * inverse).astype(BF16)


def rest_kernel(inverse, rows, tokens_ref, weight_ref, third_lo_ref, third_hi_ref, own_ref):
    plane = lax.axis_index("tensor")
    third = product_rows(tokens_ref, weight_ref, third_block(plane), rows, inverse)
    cut = third_lo_ref.shape[0]
    third_lo_ref[...] = third[:cut]
    third_hi_ref[...] = third[cut:]
    own_ref[...] = product_rows(tokens_ref, weight_ref, plane, rows, inverse)


def relay_kernel(third_lo_ref, third_hi_ref, near_ref, seed_ref, out_ref):
    outer = is_outer(lax.axis_index("tensor"))
    cut = third_lo_ref.shape[0]

    @pl.when(outer)
    def _():
        out_ref[...] = near_ref[...]

    @pl.when(jnp.logical_not(outer))
    def _():
        for span, ref in ((slice(0, cut), third_lo_ref), (slice(cut, None), third_hi_ref)):
            total = ref[...].astype(F32) + seed_ref[span, :].astype(F32)
            out_ref[span, :] = total.astype(BF16)


def momentum_kernel(step, share, tokens_ref, cot_ref, old_ref, fresh_ref, send_ref, keep_ref):
    odd = lax.axis_index("dp") % 2 == 1
    depth, width = fresh_ref.shape
    for k in range(depth // TILE):
        rows = slice(k * TILE, (k + 1) * TILE)
        turned = tokens_ref[:, rows].T
        for pair in range(width // (2 * share)):
            span = slice(2 * pair * share, 2 * (pair + 1) * share)
            gradient = jnp.dot(turned, cot_ref[:, span], preferred_element_type=F32)
            fresh = (0.9 * old_ref[0, rows, span].astype(F32) + step * gradient).astype(BF16)
            fresh_ref[rows, span] = fresh
            votes = jnp.clip(fresh * BF16(8), BF16(-1), BF16(1))
            low, high = votes[:, :share], votes[:, share:]
            send_ref[pair, rows] = jnp.where(odd, low, high)
            keep_ref[pair, rows] = jnp.where(odd, high, low)


def back_kernel(inverse, cot_ref, weight_ref, fresh_ref, back, new, back_ref, sems):
    store = pltpu.make_async_copy(fresh_ref, new.at[0], sems.at[0])
    store.start()
    rows = cot_ref.shape[0] // 2
    stores = [store]
    for k in range(2):
        span = pl.ds(k * rows, rows)
        total = lax.dot_general(
            cot_ref[k * rows : (k + 1) * rows, :],
            weight_ref[...],
            (((1,), (1,)), ((), ())),
            preferred_element_type=F32,
        )
        back_ref[k * rows : (k + 1) * rows, :] = (total * inverse).astype(BF16)
        stores.append(pltpu.make_async_copy(back_ref.at[span], back.at[span], sems.at[1 + k]))
        stores[-1].start()
    for store in stores:
        store.wait()


def pair_kernel(keep_ref, came_ref, *out_refs):
    place = lax.axis_index("dp")
    for step, out_ref in enumerate(out_refs):
        there = jnp.bitwise_xor(place // 2, chip_offset(place, step))
        total = keep_ref[there].astype(F32) + came_ref[there].astype(F32)
        out_ref[...] = total.astype(BF16)


def chip_offset(place, step):
    return step if step in (0, 3) else 1 + (step - 1 + place) % 2


def update_kernel(share, weight_ref, threshold_ref, *refs):
    vote_refs, out_ref = refs[:-1], refs[-1]
    first = pl.multiple_of(lax.axis_index("dp") * share, share)
    votes = vote_refs[0][...].astype(F32)
    for ref in vote_refs[1:]:
        votes = votes + ref[...].astype(F32)
    limits = threshold_ref[:, pl.ds(first, share)].astype(F32)
    update = jnp.clip(votes / limits, -1.0, 1.0)
    old = weight_ref[:, pl.ds(first, share)].astype(F32)
    out_ref[...] = (old - 0.5 * update).astype(BF16)


def keys_kernel(
    own_ref,
    seed_ref,
    cross_ref,
    cycle_lo_ref,
    cycle_hi_ref,
    last_ref,
    updated_ref,
    keys,
    new_weight,
    keys_ref,
    sems,
):
    weight_copy = pltpu.make_async_copy(updated_ref, new_weight, sems.at[0])
    weight_copy.start()
    outer = is_outer(lax.axis_index("tensor"))
    total = own_ref[...].astype(F32) + last_ref[...].astype(F32)

    @pl.when(outer)
    def _():
        keys_ref[...] = (total + seed_ref[...].astype(F32)).astype(BF16)

    @pl.when(jnp.logical_not(outer))
    def _():
        cut = cycle_lo_ref.shape[0]
        for span, ref in ((slice(0, cut), cycle_lo_ref), (slice(cut, None), cycle_hi_ref)):
            more = cross_ref[span, :].astype(F32) + ref[...].astype(F32)
            keys_ref[span, :] = (total[span] + more).astype(BF16)

    keys_copy = pltpu.make_async_copy(keys_ref, keys, sems.at[1])
    keys_copy.start()
    weight_copy.wait()
    keys_copy.wait()


def in_hbm(array):
    return pltpu.with_memory_space_constraint(array, pltpu.HBM)


def call(kernel, bound, outs, args, in_specs=None, out_specs=None, scratch=(), limit=VMEM_LIMIT):
    def body(*refs):
        kernel(*bound, *refs)

    return pl.pallas_call(
        body,
        out_shape=outs,
        in_specs=in_specs or [IN_VMEM] * len(args),
        out_specs=out_specs or [IN_VMEM] * len(outs),
        scratch_shapes=scratch,
        compiler_params=pltpu.CompilerParams(vmem_limit_bytes=limit),
    )(*args)


def on_line_of_four(tokens, cotangent, weight, momentum, threshold):
    depth, width = weight.shape
    n_dp, n_tensor = lax.axis_size("dp"), lax.axis_size("tensor")
    n_chips = n_dp // 2
    rows = tokens.shape[0] // n_tensor
    share = width // n_dp
    inverse = (depth * n_tensor) ** (-0.5)
    dma = pltpu.SemaphoreType.DMA

    def along(value, goal):
        pairs = []
        for d in range(n_dp):
            for plane in range(n_tensor):
                to = goal[plane]
                there = d * n_tensor + to if to is not None else (d ^ 1) * n_tensor + plane
                pairs.append((d * n_tensor + plane, there))
        return lax.ppermute(value, ("dp", "tensor"), pairs)

    def over(value, goal):
        return lax.ppermute(value, "dp", [(i, goal(i)) for i in range(n_dp)])

    block = shaped(rows, width)
    cut = rows * 11 // 16
    halves = [shaped(cut, width), shaped(rows - cut, width)]
    seed, near, tokens, weight, cotangent = call(
        first_kernel,
        (inverse, rows),
        [block, block, shaped(*tokens.shape), shaped(*weight.shape), shaped(*cotangent.shape)],
        (in_hbm(tokens), in_hbm(weight), in_hbm(cotangent)),
        in_specs=[IN_HBM] * 3,
        scratch=[dma((5 + depth // TILE,))],
    )
    seed_came = along(seed, (1, 0, 3, 2))
    cross_came = along(near, (None, 2, 1, None))

    votes_shape = shaped(n_chips, depth, share)
    fresh, send, keep = call(
        momentum_kernel,
        (0.1 * inverse, share),
        [shaped(depth, width), votes_shape, votes_shape],
        (tokens, cotangent, momentum),
    )
    came = over(send, lambda i: i ^ 1)

    third_lo, third_hi, own = call(rest_kernel, (inverse, rows), halves + [block], (tokens, weight))
    lo_came = along(third_lo, (2, 0, 3, 1))
    hi_came = along(third_hi, (2, 0, 3, 1))

    sums = call(pair_kernel, (), [shaped(depth, share)] * n_chips, (keep, came))
    votes = [sums[0]] + [
        over(sums[k], lambda i, k=k: i ^ (2 * chip_offset(i, k)))
        for k in range(1, n_chips)
    ]

    (relay,) = call(relay_kernel, (), [block], (third_lo, third_hi, near, seed_came))
    last_came = along(relay, (1, 3, 0, 2))

    input_grad, new_momentum = call(
        back_kernel,
        (inverse,),
        [shaped(*tokens.shape), shaped(1, depth, width)],
        (cotangent, weight, fresh),
        out_specs=[IN_HBM] * 2,
        scratch=[pltpu.VMEM(tokens.shape, BF16), dma((3,))],
    )
    (updated,) = call(
        update_kernel,
        (share,),
        [shaped(depth, share)],
        (weight, threshold.reshape(1, width)) + tuple(votes),
    )
    key_values, new_weight = call(
        keys_kernel,
        (),
        [block, shaped(depth, share)],
        (own, seed_came, cross_came, lo_came, hi_came, last_came, updated),
        out_specs=[IN_HBM] * 2,
        scratch=[pltpu.VMEM((rows, width), BF16), dma((2,))],
    )
    return key_values, input_grad, new_momentum, new_weight


def in_general(tokens, cotangent, weight, momentum, threshold):
    inverse = (weight.shape[0] * lax.axis_size("tensor")) ** (-0.5)
    key_values = lax.psum_scatter(
        (jnp.dot(tokens, weight, preferred_element_type=F32) * inverse).astype(BF16),
        "tensor",
        scatter_dimension=0,
        tiled=True,
    )
    input_grad = (
        lax.dot_general(cotangent, weight, (((1,), (1,)), ((), ())), preferred_element_type=F32)
        * inverse
    ).astype(BF16)
    gradient = inverse * lax.dot_general(
        tokens, cotangent, (((0,), (0,)), ((), ())), preferred_element_type=F32
    )
    fresh = (0.9 * momentum[0].astype(F32) + 0.1 * gradient).astype(BF16)
    share = weight.shape[1] // lax.axis_size("dp")
    arrived = lax.all_to_all(fresh[None], "dp", split_axis=2, concat_axis=0, tiled=True)
    votes = jnp.sum(jnp.clip(arrived.astype(F32) / 0.125, -1.0, 1.0), axis=0)
    first = lax.axis_index("dp") * share
    own_columns = lax.dynamic_slice_in_dim(weight, first, share, 1)
    own_limits = lax.dynamic_slice_in_dim(threshold, first, share, 0)
    update = jnp.clip(votes / own_limits.astype(F32)[None, :], -1.0, 1.0)
    new_weight = (own_columns.astype(F32) - 0.5 * update).astype(BF16)
    return key_values, input_grad, fresh[None], new_weight


def solution(mesh):
    n_dp, n_tensor = mesh.shape["dp"], mesh.shape["tensor"]

    def per_device(tokens, cotangent, weight, momentum, threshold):
        depth, width = weight.shape
        fits = n_tensor == 4 and n_dp == 8 and width % (n_dp * LANES) == 0
        fits = fits and depth % TILE == 0 and tokens.shape[0] % (64 * n_tensor) == 0
        chosen = on_line_of_four if fits else in_general
        return chosen(tokens, cotangent, weight, momentum, threshold)

    in_specs = (P("dp", "tensor"), P("dp", None), P("tensor", None), P("dp", "tensor", None), P())
    out_specs = (
        P(("dp", "tensor"), None),
        P("dp", "tensor"),
        P("dp", "tensor", None),
        P("tensor", "dp"),
    )
    return jax.shard_map(
        per_device, mesh=mesh, in_specs=in_specs, out_specs=out_specs, check_vma=False
    )
```
